256 devices in a mesh: chan: 16 (over x, y), kin: 16 (over z, core).
Axes of the slice: x: 4, y: 4, z: 8, core: 2. Of those that a mesh axis runs over, the one named last changes fastest.
Arguments:
- amplitudes: bfloat16 [2048, 512, 512], P(('chan', 'kin')), may hold values from -0.25 to 0.25
- coulomb: bfloat16 [2048, 512, 512], P(('chan', 'kin')), may hold values from -6 to 6
- energies: float32 [2048, 512], P(('chan', 'kin')), may hold values from 0.5 to 3
- orders: int32 [2048], P(('chan', 'kin')), may hold values from 384 to 512, as said below
- partner: int32 [2048], P(('chan', 'kin')), may hold values from 0 to 2047, as said below
- listed: int32 [8192], P(('chan', 'kin')), may hold values from 0 to 122, as said below
- mate_piece: int32 [8192], P(('chan', 'kin')), may hold values from 0 to 511, as said below
Outputs:
- updated: bfloat16 [2048, 512, 512], P(('chan', 'kin'))
The draws below stay inside these ranges and needn't reach their ends.
Inputs may be any that keep to these rules, and one draw needn't show every extreme that they name: `orders`: each channel's order is one of 384, 448 and 512; a channel and its partner have the same order. partner is an involution without fixed points; the partner of a channel held by the device with chan index i and kin index k is held by the device with chan index i xor (8) and the same kin index. `listed`: the 32 entries of one device are distinct tiles whose tile row and tile column are both below 3. `mate_piece`: the mate relation is an involution without fixed points among the listed pieces of the devices of one chan index; at most 4 pieces of one device have their mates on any one device (itself included), and in every chan index some pair of devices reaches 4.
All inputs are finite; a program needn't handle non-finite values.
Results may differ from the reference program's by a relative error of at most 0.006.
Values may be sent and summed in bfloat16 or wider, within the bound.
No kernel may reach another device: no remote copies, remote signals or barrier semaphores. Data moves between devices by JAX's collectives and lax.ppermute only.
A program may use at most 128 MiB of HBM per device.

```python
import math
import jax
import jax.numpy as jnp
from jax import lax

NMAX = 512
TILE = 128
CH_DEV = 8
PIECES = 32
CHANNELS = 2048
N_CHAN = 16
N_KIN = 16


def channel_tables(key):
    half_chan = N_CHAN // 2
    groups = half_chan * N_KIN
    subkeys = jax.random.split(jax.random.fold_in(key, 11), groups)
    pairing = jax.vmap(lambda subkey: jax.random.permutation(subkey, CH_DEV))(subkeys).astype(jnp.int32)
    inverse = jnp.argsort(pairing, axis=1).astype(jnp.int32)
    levels = jax.random.randint(jax.random.fold_in(key, 12), (groups, CH_DEV), 0, 3).astype(jnp.int32)
    levels = levels.at[0, 0].set(0)
    levels = levels.at[0, 1].set(2)
    channel = jnp.arange(CHANNELS, dtype=jnp.int32)
    device = channel // CH_DEV
    slot_index = channel % CH_DEV
    chan_row = device // N_KIN
    kin_index = device % N_KIN
    upper = chan_row >= half_chan
    group_index = chan_row % half_chan * N_KIN + kin_index
    mate_row = jnp.where(upper, chan_row - half_chan, chan_row + half_chan)
    mate_slot = jnp.where(upper, inverse[group_index, slot_index], pairing[group_index, slot_index])
    partner_channel = (mate_row * N_KIN + kin_index) * CH_DEV + mate_slot
    lower_slot = jnp.where(upper, inverse[group_index, slot_index], slot_index)
    order_value = NMAX - levels[group_index, lower_slot] * (NMAX // 8)
    return (order_value.astype(jnp.int32), partner_channel.astype(jnp.int32))


def draw_orders(key, part):
    return channel_tables(key)[0]


def draw_partner(key, part):
    return channel_tables(key)[1]


def piece_tables(key):
    devices = N_CHAN * N_KIN
    valid_count = CH_DEV * 9
    subkeys = jax.random.split(jax.random.fold_in(key, 21), devices)
    choose = jax.vmap(lambda subkey: jax.random.permutation(subkey, valid_count)[:PIECES])(subkeys).astype(jnp.int32)
    listed_tiles = choose // 9 * 16 + choose % 9 // 3 * 4 + choose % 3
    order_keys = jax.random.split(jax.random.fold_in(key, 22), devices)
    placing = jax.vmap(lambda subkey: jax.random.permutation(subkey, PIECES))(order_keys).astype(jnp.int32)
    split_draw = jax.random.randint(jax.random.fold_in(key, 23), (N_CHAN, N_KIN // 2), 0, 3).astype(jnp.int32) * 2
    leading = jax.random.randint(jax.random.fold_in(key, 24), (N_CHAN,), 0, 2).astype(jnp.int32) * 4
    split_draw = split_draw.at[:, 0].set(leading)
    lane_sizes = jnp.stack([split_draw, 4 - split_draw], axis=2).reshape(N_CHAN, N_KIN)
    lane_end = jnp.cumsum(lane_sizes, axis=1).astype(jnp.int32)
    lane_first = lane_end - lane_sizes
    device = jnp.arange(devices, dtype=jnp.int32)
    chan_row = device // N_KIN
    kin_index = device % N_KIN
    position = jnp.arange(PIECES, dtype=jnp.int32)
    lane_index = jnp.sum((lane_end[chan_row][:, None, :] <= position[None, :, None]).astype(jnp.int32), axis=2).astype(jnp.int32)
    lane_start = jnp.take_along_axis(lane_first[chan_row], lane_index, axis=1)
    offset = position[None, :] - lane_start
    peer_kin = (lane_index - kin_index[:, None]) % N_KIN
    mate_offset = jnp.where(peer_kin == kin_index[:, None], offset + 1 - 2 * (offset % 2), offset)
    mate_position = lane_start + mate_offset
    mate_device = chan_row[:, None] * N_KIN + peer_kin
    mate_index = placing[mate_device, mate_position]
    mate_value = (peer_kin * PIECES + mate_index).astype(jnp.int32)
    mate_table = jnp.zeros((devices, PIECES), jnp.int32)
    mate_table = mate_table.at[device[:, None], placing].set(mate_value)
    return (listed_tiles.reshape(-1).astype(jnp.int32), mate_table.reshape(-1).astype(jnp.int32))


def draw_listed(key, part):
    return piece_tables(key)[0]


def draw_mate_piece(key, part):
    return piece_tables(key)[1]


def block_levels(own_key, shape, shards, smallest, high):
    def one(axis_at, blocks):
        draws = jax.random.uniform(jax.random.fold_in(jax.random.fold_in(own_key, 6), axis_at), (blocks,), jnp.float32, smallest / len(shards), high / len(shards))
        return jnp.repeat(jnp.exp(draws), shape[axis_at] // blocks).reshape((-1,) + (1,) * (len(shape) - axis_at - 1))

    level = one(*shards[0])
    for cut in shards[1:]:
        level = level * one(*cut)
    return level


def centred(key, shape, spread, most, cuts=(), kind=jnp.bfloat16):
    array = spread * jax.random.normal(key, shape, jnp.float32)
    if cuts:
        array = array * block_levels(key, shape, cuts, -0.22, 0.18)
    return jnp.clip(array, -most, most).astype(kind)


def setup_inputs(seed: int = 0) -> dict:
    seeds = jax.random.split(jax.random.key(seed), 8)
    amplitudes = centred(seeds[0], (CHANNELS, NMAX, NMAX), NMAX ** -0.5, 0.25, ((0, 256),))
    coulomb = centred(seeds[1], (CHANNELS, NMAX, NMAX), 1.0, 6.0, ((0, 256),))
    energies = jnp.clip(jnp.exp(math.log(3.0) - 1.7917595 * jax.random.uniform(seeds[2], (CHANNELS, NMAX), jnp.float32) ** block_levels(seeds[2], (CHANNELS, NMAX), ((0, 256),), -0.2, 0.2)), 0.5, 3.0)
    orders = draw_orders(jax.random.fold_in(seeds[7], 71), 0)
    partner = draw_partner(jax.random.fold_in(seeds[7], 71), 0)
    listed = draw_listed(jax.random.fold_in(seeds[7], 71), 0)
    mate_piece = draw_mate_piece(jax.random.fold_in(seeds[7], 71), 0)
    return dict(amplitudes=amplitudes, coulomb=coulomb, energies=energies, orders=orders, partner=partner, listed=listed, mate_piece=mate_piece)


def block_mask(order_value):
    indices = jnp.arange(NMAX, dtype=jnp.int32)
    inside = indices < order_value
    return inside[:, None] & inside[None, :]


def cycle_residual(operands):
    amp_block, coul_block, order_value = operands
    keep_mask = block_mask(order_value)
    amp_kept = jnp.where(keep_mask, amp_block, jnp.zeros_like(amp_block))
    coul_kept = jnp.where(keep_mask, coul_block, jnp.zeros_like(coul_block))
    forward = jnp.dot(amp_kept, coul_kept, preferred_element_type=jnp.float32)
    forward_half = forward.astype(jnp.bfloat16)
    backward = jnp.dot(coul_kept, amp_kept, preferred_element_type=jnp.float32)
    sandwich = jnp.dot(forward_half, amp_kept, preferred_element_type=jnp.float32)
    return (coul_kept.astype(jnp.float32) + backward + forward + sandwich).astype(jnp.bfloat16)


def reference(amplitudes, coulomb, energies, orders, partner, listed, mate_piece):
    residual = lax.map(cycle_residual, (amplitudes, coulomb, orders))

    def symmetrize(operands):
        own_block, partner_index = operands
        mirror = lax.dynamic_index_in_dim(residual, partner_index.astype(jnp.int32), 0, keepdims=False)
        total = 0.5 * (own_block.astype(jnp.float32) + mirror.T.astype(jnp.float32))
        return total.astype(jnp.bfloat16)

    coupled = lax.map(symmetrize, (residual, partner))
    channels = coupled.shape[0]
    tile_stack = coupled.reshape(channels, 4, TILE, 4, TILE).transpose(0, 1, 3, 2, 4).reshape(channels * 16, TILE, TILE)
    piece_ids = jnp.arange(listed.shape[0], dtype=jnp.int32)
    owner_device = piece_ids // PIECES
    tile_ids = ((owner_device * CH_DEV + listed // 16) * 16 + listed % 16).astype(jnp.int32)
    mate_ids = ((owner_device // N_KIN) * (N_KIN * PIECES) + mate_piece).astype(jnp.int32)
    piece_tiles = tile_stack[tile_ids]
    mate_tiles = piece_tiles[mate_ids]
    exchanged = tile_stack.astype(jnp.float32).at[tile_ids].add(-jnp.swapaxes(mate_tiles, 1, 2).astype(jnp.float32))
    unfolded = exchanged.reshape(channels, 4, 4, TILE, TILE).transpose(0, 1, 3, 2, 4).reshape(channels, NMAX, NMAX)

    def finish(operands):
        unfolded_block, energy_row, order_value = operands
        denominator = energy_row[:, None] + energy_row[None, :]
        return jnp.where(block_mask(order_value), unfolded_block / denominator, jnp.zeros_like(unfolded_block)).astype(jnp.bfloat16)

    return lax.map(finish, (unfolded, energies, orders))
```

```python
import functools

import jax
import jax.numpy as jnp
from jax import lax
from jax.experimental import pallas as pl
from jax.experimental.pallas import tpu as pltpu
from jax.sharding import PartitionSpec as P


CAP = 4
INNER = 3
PER_STEP = 2
BF = jnp.bfloat16
F32 = jnp.float32
ANY = pl.BlockSpec(memory_space=pl.ANY)
WHOLE = pl.BlockSpec(memory_space=pltpu.VMEM)
SMALL = pltpu.CompilerParams(vmem_limit_bytes=6 << 20)


def shell_base(orders, slot, edge, half):
    base = jnp.int32(0)
    for other in range(orders.shape[0]):
        base += jnp.where(other < slot, (orders[other] - edge) // half, 0)
    return base


def residual_channel(orders, amp, coul, lane, slot, own, shell_own):
    block = amp.shape[1]
    tile = block // 4
    half = tile // 2
    edge = INNER * tile
    order = orders[slot]
    rows = lax.broadcasted_iota(jnp.int32, (block, block), 0)
    cols = lax.broadcasted_iota(jnp.int32, (block, block), 1)
    keep = jnp.maximum(rows, cols) < order
    t_kept = jnp.where(keep, amp[lane], jnp.zeros_like(amp[lane]))
    v_kept = jnp.where(keep, coul[lane], jnp.zeros_like(coul[lane]))
    right = v_kept.astype(F32) + jnp.dot(v_kept, t_kept, preferred_element_type=F32)
    both = right + jnp.dot(t_kept, right.astype(BF), preferred_element_type=F32)
    both = both.astype(BF)
    own[slot] = both
    for cut in range(2):
        for col in range(INNER + 1):
            shell_own[slot, cut, col * half : (col + 1) * half] = both[
                edge + cut * half : edge + (cut + 1) * half, col * tile : (col + 1) * tile
            ]
    for row in range(INNER):
        side = both[row * tile : (row + 1) * tile, edge:].T
        for cut in range(2):
            low = (INNER + 1 + row) * half
            shell_own[slot, cut, low : low + half] = side[cut * half : (cut + 1) * half]


def send_channel(orders, slot, own, shell_own, res, shells, res_sem, shell_sem, wait):
    tile = own.shape[1] // 4
    half = tile // 2
    edge = INNER * tile
    whole = pltpu.make_async_copy(own.at[slot], res.at[slot], res_sem.at[slot])
    whole.wait() if wait else whole.start()
    base = jnp.int32(0) if wait else shell_base(orders, slot, edge, half)
    for cut in range(2):
        @pl.when((orders[slot] - edge) // half > cut)
        def _():
            copy = pltpu.make_async_copy(
                shell_own.at[slot, cut], shells.at[base + cut], shell_sem.at[slot, cut]
            )
            copy.wait() if wait else copy.start()


def early_kernel(orders, amp, coul, res, shells, own, shell_own, res_sem, shell_sem):
    step = pl.program_id(0)
    for lane in range(PER_STEP):
        residual_channel(orders, amp, coul, lane, step * PER_STEP + lane, own, shell_own)
    for lane in range(PER_STEP):
        send_channel(orders, step * PER_STEP + lane, own, shell_own, res, shells, res_sem, shell_sem, False)

    @pl.when(step == pl.num_programs(0) - 1)
    def _():
        for slot in range(own.shape[0]):
            send_channel(orders, slot, own, shell_own, res, shells, res_sem, shell_sem, True)


def late_kernel(
    orders, partner, wanted, amp, coul, res_in, shells_in, res, shells, first, second,
    own, shell_own, place, back, res_sem, shell_sem, load_sem, first_sem, second_sem,
):
    del shells_in
    channels = own.shape[0]
    early = channels // 2
    pieces = first.shape[0]
    tile = first.shape[1]
    inner = INNER * INNER
    step = pl.program_id(0)
    load = pltpu.make_async_copy(res_in.at[pl.ds(0, early)], own.at[pl.ds(0, early)], load_sem)

    @pl.when(step == 0)
    def _():
        load.start()
        for slot in range(channels):
            back[partner[slot] % channels] = slot

        def clear(t, carry):
            place[t] = -1
            return carry

        lax.fori_loop(0, channels * inner, clear, 0, unroll=8)

        def mark(p, carry):
            code = wanted[p]
            row = (code % 16) // 4
            col = code % 4
            place[back[code // 16] * inner + col * INNER + row] = p
            return carry

        lax.fori_loop(0, pieces, mark, 0, unroll=4)

        def rank(t, count):
            listed = place[t] >= 0
            place[t] = jnp.where(listed, place[t], pieces + count)
            return count + jnp.where(listed, 0, 1)

        lax.fori_loop(0, channels * inner, rank, 0, unroll=8)

    for lane in range(PER_STEP):
        residual_channel(orders, amp, coul, lane, early + step * PER_STEP + lane, own, shell_own)

    def send_tiles(slot):
        for row in range(INNER):
            for col in range(INNER):
                where = place[slot * inner + row * INNER + col]
                source = own.at[slot, pl.ds(row * tile, tile), pl.ds(col * tile, tile)]

                @pl.when(where < pieces)
                def _():
                    pltpu.make_async_copy(source, first.at[where], first_sem).start()

                @pl.when(where >= pieces)
                def _():
                    pltpu.make_async_copy(source, second.at[where - pieces], second_sem).start()

    for lane in range(PER_STEP):
        send_tiles(early + step * PER_STEP + lane)
    for lane in range(PER_STEP):
        send_channel(
            orders, early + step * PER_STEP + lane, own, shell_own, res, shells, res_sem, shell_sem, False
        )

    @pl.when(step == 0)
    def _():
        load.wait()

        def body(slot, carry):
            send_tiles(slot)
            return carry

        lax.fori_loop(0, early, body, 0)

    @pl.when(step == pl.num_programs(0) - 1)
    def _():
        for slot in range(early, channels):
            send_channel(orders, slot, own, shell_own, res, shells, res_sem, shell_sem, True)
        pltpu.make_async_copy(first, first, first_sem).wait()
        pltpu.make_async_copy(second, second, second_sem).wait()


def residuals(orders, partner, wanted, amp, coul):
    channels, block, _ = amp.shape
    tile = block // 4
    early = channels // 2
    pieces = wanted.shape[0]
    rest = channels * INNER * INNER - pieces
    steps = early // PER_STEP
    res_shape = jax.ShapeDtypeStruct((channels, block, block), BF)
    shell_shape = jax.ShapeDtypeStruct((2 * channels, 7 * tile // 2, tile), BF)
    cost = pl.CostEstimate(
        flops=early * 4 * block**3, bytes_accessed=early * block * block * 8, transcendentals=0
    )

    def scratch(rows):
        return [
            pltpu.VMEM((rows, block, block), BF),
            pltpu.VMEM((rows, 2, 7 * tile // 2, tile), BF),
        ]

    spec = pl.BlockSpec((PER_STEP, block, block), lambda s, *_: (s, 0, 0))
    res, shells = pl.pallas_call(
        early_kernel,
        out_shape=(res_shape, shell_shape),
        grid_spec=pltpu.PrefetchScalarGridSpec(
            num_scalar_prefetch=1,
            grid=(steps,),
            in_specs=[spec, spec],
            out_specs=(ANY, ANY),
            scratch_shapes=scratch(early)
            + [pltpu.SemaphoreType.DMA((early,)), pltpu.SemaphoreType.DMA((early, 2))],
        ),
        cost_estimate=cost,
        name="early",
    )(orders, amp, coul)
    spec = pl.BlockSpec((PER_STEP, block, block), lambda s, *_: (s + steps, 0, 0))
    return pl.pallas_call(
        late_kernel,
        out_shape=(
            res_shape,
            shell_shape,
            jax.ShapeDtypeStruct((pieces, tile, tile), BF),
            jax.ShapeDtypeStruct((rest, tile, tile), BF),
        ),
        grid_spec=pltpu.PrefetchScalarGridSpec(
            num_scalar_prefetch=3,
            grid=(steps,),
            in_specs=[spec, spec, ANY, ANY],
            out_specs=(ANY, ANY, ANY, ANY),
            scratch_shapes=scratch(channels)
            + [
                pltpu.SMEM((channels * INNER * INNER,), jnp.int32),
                pltpu.SMEM((channels,), jnp.int32),
                pltpu.SemaphoreType.DMA((channels,)),
                pltpu.SemaphoreType.DMA((channels, 2)),
                pltpu.SemaphoreType.DMA(()),
                pltpu.SemaphoreType.DMA(()),
                pltpu.SemaphoreType.DMA(()),
            ],
        ),
        input_output_aliases={5: 0, 6: 1},
        cost_estimate=cost,
        name="late",
    )(orders, partner, wanted, amp, coul, res, shells)


def column_of(row, tile):
    return jnp.broadcast_to(row, (tile, tile)).T


def prepare_kernel(listed, energy, res, held, inverse, mine):
    step = pl.program_id(0)
    tile = mine.shape[1]
    across = energy[pl.ds(step, 1), :]
    held[step] = res[0]
    for row in range(INNER + 1):
        down = column_of(across[:, row * tile : (row + 1) * tile], tile)
        for col in range(INNER + 1):
            inverse[step, row * tile : (row + 1) * tile, col * tile : (col + 1) * tile] = 1.0 / (
                down + across[:, col * tile : (col + 1) * tile]
            )

    @pl.when(step == pl.num_programs(0) - 1)
    def _():
        def body(p, carry):
            code = listed[p]
            row = pl.multiple_of((code % 16) // 4 * tile, tile)
            col = pl.multiple_of(code % 4 * tile, tile)
            mine[p] = held[code // 16, pl.ds(row, tile), pl.ds(col, tile)]
            return carry

        lax.fori_loop(0, mine.shape[0], body, 0, unroll=4)


def prepare(listed, energies, res):
    channels, block, _ = res.shape
    tile = block // 4
    return pl.pallas_call(
        prepare_kernel,
        out_shape=(
            jax.ShapeDtypeStruct(res.shape, BF),
            jax.ShapeDtypeStruct(res.shape, F32),
            jax.ShapeDtypeStruct((listed.shape[0], tile, tile), BF),
        ),
        grid_spec=pltpu.PrefetchScalarGridSpec(
            num_scalar_prefetch=1,
            grid=(channels,),
            in_specs=[WHOLE, pl.BlockSpec((1, block, block), lambda s, *_: (s, 0, 0))],
            out_specs=(WHOLE, WHOLE, WHOLE),
        ),
        compiler_params=pltpu.CompilerParams(vmem_limit_bytes=20 << 20),
        name="prepare",
    )(listed, energies, res)


def coupled(own, other):
    return (own + other) * jnp.asarray(0.5, BF)


def couple_kernel(table, mine, theirs, pairs, *outgoing):
    pieces = mine.shape[0]

    def body(p, carry):
        pairs[p] = coupled(mine[p], theirs[p].T)
        return carry

    lax.fori_loop(0, pieces, body, 0, unroll=8)
    for hop, out in enumerate(outgoing):
        for slot in range(CAP):
            out[slot] = pairs[jnp.maximum(table[hop * CAP + slot], 0)]


def couple(table, mine, theirs, peers):
    pieces, tile, _ = mine.shape
    part = jax.ShapeDtypeStruct((CAP, tile, tile), BF)
    return pl.pallas_call(
        couple_kernel,
        out_shape=(jax.ShapeDtypeStruct((pieces, tile, tile), BF),) + (part,) * peers,
        grid_spec=pltpu.PrefetchScalarGridSpec(
            num_scalar_prefetch=1, in_specs=[WHOLE, WHOLE], out_specs=(WHOLE,) * (1 + peers)
        ),
        compiler_params=SMALL,
        name="couple",
    )(table, mine, theirs)


def rest_kernel(orders, spot, base, held, inverse, second, shells, out):
    step = pl.program_id(0)
    tile = second.shape[1]
    half = tile // 2
    inner = INNER * INNER
    edge = INNER * tile
    shell_count = shells.shape[0]
    order = orders[step]

    def put(row, col, other):
        rows = slice(row * tile, (row + 1) * tile)
        cols = slice(col * tile, (col + 1) * tile)
        value = coupled(held[step, rows, cols], other).astype(F32) * inverse[step, rows, cols]
        if max(row, col) == INNER:
            down = lax.broadcasted_iota(jnp.int32, (tile, tile), 0) + row * tile
            across = lax.broadcasted_iota(jnp.int32, (tile, tile), 1) + col * tile
            value = jnp.where(jnp.maximum(down, across) < order, value, 0.0)
        out[0, rows, cols] = value.astype(BF)

    for row in range(INNER):
        for col in range(INNER):
            put(row, col, second[spot[step * inner + row * INNER + col]].T)

    @pl.when(order > edge)
    def _():
        low = jnp.minimum(base[step], shell_count - 1)
        high = jnp.minimum(base[step] + 1, shell_count - 1)

        def joined(unit):
            window = pl.ds(unit * half, half)
            return jnp.concatenate([shells[low, window], shells[high, window]], axis=0)

        for row in range(INNER + 1):
            put(row, INNER, joined(row).T)
        for col in range(INNER):
            put(INNER, col, joined(INNER + 1 + col))

    @pl.when(order <= edge)
    def _():
        out[0, edge:, :] = jnp.zeros((tile, out.shape[2]), BF)
        out[0, :edge, edge:] = jnp.zeros((edge, tile), BF)


def finish_rest(orders, spot, base, held, inverse, second, shells):
    channels, block, _ = held.shape
    return pl.pallas_call(
        rest_kernel,
        out_shape=jax.ShapeDtypeStruct(held.shape, BF),
        grid_spec=pltpu.PrefetchScalarGridSpec(
            num_scalar_prefetch=3,
            grid=(channels,),
            in_specs=[WHOLE, WHOLE, WHOLE, WHOLE],
            out_specs=pl.BlockSpec((1, block, block), lambda s, *_: (s, 0, 0)),
        ),
        compiler_params=SMALL,
        name="rest",
    )(orders, spot, base, held, inverse, second, shells)


def listed_kernel(peers, listed, table, pairs, inverse, *refs):
    incoming, (_, out, mates, made, sem) = refs[:peers], refs[peers:]
    pieces, tile, _ = pairs.shape
    for hop, part in enumerate(incoming):
        for slot in range(CAP):
            piece = table[hop * CAP + slot]
            mates[jnp.where(piece < 0, pieces, piece)] = part[slot]

    def body(p, carry):
        code = listed[p]
        channel = code // 16
        rows = pl.ds(pl.multiple_of((code % 16) // 4 * tile, tile), tile)
        cols = pl.ds(pl.multiple_of(code % 4 * tile, tile), tile)
        value = pairs[p].astype(F32) - mates[p].T.astype(F32)
        made[p] = (value * inverse[channel, rows, cols]).astype(BF)
        pltpu.make_async_copy(made.at[p], out.at[channel, rows, cols], sem).start()
        return carry

    lax.fori_loop(0, pieces, body, 0, unroll=8)
    pltpu.make_async_copy(made, made, sem).wait()


def finish_listed(listed, table, pairs, inverse, incoming, prior):
    pieces, tile, _ = pairs.shape
    peers = len(incoming)
    return pl.pallas_call(
        functools.partial(listed_kernel, peers),
        out_shape=jax.ShapeDtypeStruct(prior.shape, BF),
        grid_spec=pltpu.PrefetchScalarGridSpec(
            num_scalar_prefetch=2,
            in_specs=[WHOLE] * (2 + peers) + [ANY],
            out_specs=ANY,
            scratch_shapes=[
                pltpu.VMEM((pieces + 1, tile, tile), BF),
                pltpu.VMEM((pieces, tile, tile), BF),
                pltpu.SemaphoreType.DMA(()),
            ],
        ),
        input_output_aliases={4 + peers: 0},
        compiler_params=SMALL,
        name="listed",
    )(listed, table, pairs, inverse, *incoming, prior)


def exchange(amplitudes, coulomb, energies, orders, partner, listed, mate_piece):
    channels, block, _ = amplitudes.shape
    tile = block // 4
    pieces = listed.shape[0]
    stride = lax.axis_size("chan") // 2
    peers = lax.axis_size("kin")
    route = [(i, i ^ stride) for i in range(2 * stride)]

    def swap(array):
        return lax.ppermute(array, "chan", route)

    wanted = swap(listed)
    res, shells, first, second = residuals(orders, partner, wanted, amplitudes, coulomb)
    first_in = swap(first)
    second_in = swap(second)
    shells_in = swap(shells)

    listed, partner, mate_piece, orders, energies, res = lax.optimization_barrier(
        (listed, partner, mate_piece, orders, energies, res)
    )
    held, inverse, mine = prepare(listed, energies, res)
    partner_slot = partner % channels
    level = (orders - INNER * tile) // (tile // 2)
    base = jnp.sum(jnp.where(partner_slot[None, :] < partner_slot[:, None], level[None, :], 0), axis=1)
    count = INNER * INNER
    tiles = jnp.arange(channels * count, dtype=jnp.int32)
    slot, row, col = tiles // count, tiles % count // INNER, tiles % INNER
    of_slot = jnp.sum(
        jnp.where(slot[:, None] == jnp.arange(channels, dtype=jnp.int32)[None, :], partner_slot[None, :], 0), axis=1
    )
    key = of_slot * count + col * INNER + row
    unlisted = jnp.all((slot * 16 + row * 4 + col)[:, None] != listed[None, :], axis=1)
    spot = jnp.sum((unlisted[None, :] & (key[None, :] < key[:, None])).astype(jnp.int32), axis=1)
    spot = jnp.minimum(spot, channels * count - pieces - 1)
    me = lax.axis_index("kin")
    target = mate_piece // pieces
    piece_index = jnp.arange(pieces, dtype=jnp.int32)
    same = target[:, None] == target[None, :]
    out_rank = jnp.sum((same & (piece_index[None, :] < piece_index[:, None])).astype(jnp.int32), axis=1)
    in_rank = jnp.sum((same & (mate_piece[None, :] < mate_piece[:, None])).astype(jnp.int32), axis=1)
    places = jnp.arange(peers * CAP, dtype=jnp.int32)

    def table_of(hop, rank):
        hit = places[:, None] == ((hop + peers) % peers * CAP + rank)[None, :]
        return jnp.sum(jnp.where(hit, piece_index[None, :] + 1, 0), axis=1) - 1

    out_table = table_of(target - me, out_rank)
    in_table = table_of(me - target, in_rank)

    pairs, *outgoing = couple(out_table, mine, first_in, peers)
    incoming = [outgoing[0]]
    for hop in range(1, peers):
        incoming.append(
            lax.ppermute(outgoing[hop], "kin", [(k, (k + hop) % peers) for k in range(peers)])
        )
    rest = finish_rest(orders, spot, base, held, inverse, second_in, shells_in)
    return finish_listed(listed, in_table, pairs, inverse, incoming, rest)


def solution(mesh):
    return jax.shard_map(
        exchange,
        mesh=mesh,
        in_specs=(
            P(("chan", "kin"), None, None),
            P(("chan", "kin"), None, None),
            P(("chan", "kin"), None),
            P(("chan", "kin")),
            P(("chan", "kin")),
            P(("chan", "kin")),
            P(("chan", "kin")),
        ),
        out_specs=P(("chan", "kin"), None, None),
        check_vma=False,
    )
```

```python
import jax
import jax.numpy as jnp
from jax import lax
from jax.experimental import pallas as pl
from jax.experimental.pallas import tpu as pltpu
from jax.sharding import PartitionSpec as P


CAP = 4
INNER = 3
PER_STEP = 2
OPENING = 2
CLOSING = 2
BF = jnp.bfloat16
F32 = jnp.float32
ANY = pl.BlockSpec(memory_space=pl.ANY)
WHOLE = pl.BlockSpec(memory_space=pltpu.VMEM)
LARGE = pltpu.CompilerParams(vmem_limit_bytes=63 << 20)
SMALL = pltpu.CompilerParams(vmem_limit_bytes=6 << 20)


def residual_channel(orders, amp, coul, lane, slot, at, own, shell_own):
    block = amp.shape[1]
    tile = block // 4
    half = tile // 2
    edge = INNER * tile
    order = orders[slot]

    def kept(array):
        cols = lax.broadcasted_iota(jnp.int32, (edge, tile), 1) + edge
        side = jnp.where(cols < order, array[:edge, edge:], jnp.zeros((edge, tile), BF))
        rows = lax.broadcasted_iota(jnp.int32, (tile, block), 0) + edge
        cols = lax.broadcasted_iota(jnp.int32, (tile, block), 1)
        low = jnp.where(jnp.maximum(rows, cols) < order, array[edge:], jnp.zeros((tile, block), BF))
        return jnp.concatenate([jnp.concatenate([array[:edge, :edge], side], axis=1), low], axis=0)

    t_kept = kept(amp[lane])
    v_kept = kept(coul[lane])
    right = v_kept.astype(F32) + jnp.dot(v_kept, t_kept, preferred_element_type=F32)
    both = right + jnp.dot(t_kept, right.astype(BF), preferred_element_type=F32)
    both = both.astype(BF)
    own[at] = both
    for cut in range(2):
        for col in range(INNER + 1):
            shell_own[at, cut, col * half : (col + 1) * half] = both[
                edge + cut * half : edge + (cut + 1) * half, col * tile : (col + 1) * tile
            ]
    for row in range(INNER):
        side = both[row * tile : (row + 1) * tile, edge:].T
        for cut in range(2):
            low = (INNER + 1 + row) * half
            shell_own[at, cut, low : low + half] = side[cut * half : (cut + 1) * half]


def send_channel(lane, slot, own, shell_own, res, shells, shell_at, res_sem, shell_sem):
    return (
        pltpu.make_async_copy(own.at[lane], res.at[slot], res_sem.at[lane]),
        pltpu.make_async_copy(shell_own.at[lane], shells.at[shell_at], shell_sem.at[lane]),
    )


def tile_of(own, lane, row, col):
    tile = own.shape[1] // 4
    return own.at[lane, pl.ds(row * tile, tile), pl.ds(col * tile, tile)]


def opening_kernel(
    orders, amp, coul, res, shells, fill, own, shell_own, res_sem, shell_sem, fill_sem
):
    for lane in range(OPENING):
        residual_channel(orders, amp, coul, lane, lane, lane, own, shell_own)
    for lane in range(OPENING):
        for row in range(INNER):
            for col in range(INNER):
                spot = (lane * INNER + row) * INNER + col
                pltpu.make_async_copy(tile_of(own, lane, row, col), fill.at[spot], fill_sem).start()
    copies = [
        copy
        for lane in range(OPENING)
        for copy in send_channel(lane, lane, own, shell_own, res, shells, lane, res_sem, shell_sem)
    ]
    for copy in copies:
        copy.start()
    for copy in copies:
        copy.wait()
    pltpu.make_async_copy(fill, fill, fill_sem).wait()


def late_kernel(
    orders, partner, wanted, amp, coul, res_in, res, shells, closing, first, second,
    own, shell_own, place, back, res_sem, shell_sem, first_sem, second_sem,
):
    del res_in
    channels = orders.shape[0]
    inner = INNER * INNER
    known = OPENING * inner
    pieces = first.shape[0]
    step = pl.program_id(0)
    last = pl.num_programs(0) - 1

    @pl.when(step == 0)
    def _():
        for slot in range(channels):
            back[partner[slot] % channels] = slot

        def clear(t, carry):
            place[t] = -1
            return carry

        lax.fori_loop(0, channels * inner, clear, 0, unroll=8)

        def mark(p, low):
            code = wanted[p]
            spot = back[code // 16] * inner + code % 4 * INNER + (code % 16) // 4
            place[spot] = low
            return low + jnp.where(spot >= known, 1, 0)

        low = lax.fori_loop(0, pieces, mark, jnp.int32(0), unroll=4)

        def rank(t, count):
            listed = place[t] >= 0
            place[t] = jnp.where(listed, place[t], count)
            return count + jnp.where(listed, 0, 1)

        lax.fori_loop(known, channels * inner, rank, low, unroll=6)

    for lane in range(PER_STEP):
        at = step * PER_STEP + lane
        residual_channel(orders, amp, coul, lane, OPENING + at, at, own, shell_own)

    def send_shells(at, target, shift):
        for copy in send_channel(
            at, OPENING + at, own, shell_own, res, target, at - shift, res_sem, shell_sem
        ):
            copy.start()

    for lane in range(PER_STEP):
        at = step * PER_STEP + lane
        for row in range(INNER):
            for col in range(INNER):
                where = place[(OPENING + at) * inner + row * INNER + col]
                source = tile_of(own, at, row, col)

                @pl.when(where < pieces)
                def _():
                    pltpu.make_async_copy(source, first.at[where], first_sem).start()

                @pl.when(where >= pieces)
                def _():
                    pltpu.make_async_copy(source, second.at[where - pieces], second_sem).start()

        @pl.when(step < last)
        def _():
            send_shells(at, shells, 0)

        @pl.when(step == last)
        def _():
            send_shells(at, closing, shells.shape[0])

    @pl.when(step == last)
    def _():
        for lane in range(channels - OPENING):
            for copy in send_channel(
                lane, OPENING + lane, own, shell_own, res, closing, 0, res_sem, shell_sem
            ):
                copy.wait()
        pltpu.make_async_copy(first, first, first_sem).wait()
        pltpu.make_async_copy(second, second, second_sem).wait()


def residuals(orders, partner, wanted, amp, coul):
    channels, block, _ = amp.shape
    tile = block // 4
    pieces = wanted.shape[0]
    known = OPENING * INNER * INNER
    rest = channels * INNER * INNER - known - pieces
    late = channels - OPENING
    res_shape = jax.ShapeDtypeStruct((channels, block, block), BF)

    def tiles(count):
        return jax.ShapeDtypeStruct((count, tile, tile), BF)

    def shell(count):
        return jax.ShapeDtypeStruct((count, 2, 7 * tile // 2, tile), BF)

    def cost(rows):
        return pl.CostEstimate(
            flops=rows * 4 * block**3, bytes_accessed=rows * block * block * 8, transcendentals=0
        )

    def scratch(rows):
        return [
            pltpu.VMEM((rows, block, block), BF),
            pltpu.VMEM((rows, 2, 7 * tile // 2, tile), BF),
        ]

    spec = pl.BlockSpec((OPENING, block, block), lambda s, *_: (0, 0, 0))
    res, shells_a, fill = pl.pallas_call(
        opening_kernel,
        out_shape=(res_shape, shell(OPENING), tiles(known)),
        grid_spec=pltpu.PrefetchScalarGridSpec(
            num_scalar_prefetch=1,
            grid=(1,),
            in_specs=[spec, spec],
            out_specs=(ANY,) * 3,
            scratch_shapes=scratch(OPENING)
            + [
                pltpu.SemaphoreType.DMA((OPENING,)),
                pltpu.SemaphoreType.DMA((OPENING,)),
                pltpu.SemaphoreType.DMA(()),
            ],
        ),
        cost_estimate=cost(OPENING),
        compiler_params=LARGE,
        name="opening",
    )(orders, amp, coul)
    shift = OPENING // PER_STEP
    spec = pl.BlockSpec((PER_STEP, block, block), lambda s, *_: (s + shift, 0, 0))
    res, shells_b, shells_c, first, second = pl.pallas_call(
        late_kernel,
        out_shape=(res_shape, shell(late - CLOSING), shell(CLOSING), tiles(pieces), tiles(rest)),
        grid_spec=pltpu.PrefetchScalarGridSpec(
            num_scalar_prefetch=3,
            grid=(late // PER_STEP,),
            in_specs=[spec, spec, ANY],
            out_specs=(ANY,) * 5,
            scratch_shapes=scratch(late)
            + [
                pltpu.SMEM((channels * INNER * INNER,), jnp.int32),
                pltpu.SMEM((channels,), jnp.int32),
                pltpu.SemaphoreType.DMA((late,)),
                pltpu.SemaphoreType.DMA((late,)),
            ]
            + [pltpu.SemaphoreType.DMA(())] * 2,
        ),
        input_output_aliases={5: 0},
        cost_estimate=cost(late),
        compiler_params=LARGE,
        name="late",
    )(orders, partner, wanted, amp, coul, res)
    return res, fill, first, second, (shells_a, shells_b, shells_c)


def column_of(row, tile):
    return jnp.broadcast_to(row, (tile, tile)).T


def prepare_kernel(listed, energy, res, held, inverse, mine):
    step = pl.program_id(0)
    tile = mine.shape[1]
    across = energy[pl.ds(step, 1), :]
    held[step] = res[0]
    for row in range(INNER + 1):
        down = column_of(across[:, row * tile : (row + 1) * tile], tile)
        for col in range(INNER + 1):
            inverse[step, row * tile : (row + 1) * tile, col * tile : (col + 1) * tile] = 1.0 / (
                down + across[:, col * tile : (col + 1) * tile]
            )

    @pl.when(step == pl.num_programs(0) - 1)
    def _():
        def body(p, carry):
            code = listed[p]
            row = pl.multiple_of((code % 16) // 4 * tile, tile)
            col = pl.multiple_of(code % 4 * tile, tile)
            mine[p] = held[code // 16, pl.ds(row, tile), pl.ds(col, tile)]
            return carry

        lax.fori_loop(0, mine.shape[0], body, 0, unroll=4)


def prepare(listed, energies, res):
    channels, block, _ = res.shape
    tile = block // 4
    return pl.pallas_call(
        prepare_kernel,
        out_shape=(
            jax.ShapeDtypeStruct(res.shape, BF),
            jax.ShapeDtypeStruct(res.shape, F32),
            jax.ShapeDtypeStruct((listed.shape[0], tile, tile), BF),
        ),
        grid_spec=pltpu.PrefetchScalarGridSpec(
            num_scalar_prefetch=1,
            grid=(channels,),
            in_specs=[WHOLE, pl.BlockSpec((1, block, block), lambda s, *_: (s, 0, 0))],
            out_specs=(WHOLE, WHOLE, WHOLE),
        ),
        compiler_params=pltpu.CompilerParams(vmem_limit_bytes=20 << 20),
        name="prepare",
    )(listed, energies, res)


def coupled(own, other):
    return (own + other) * jnp.asarray(0.5, BF)


def couple_kernel(table, spot, mine, fill, first, pairs, *refs):
    outgoing, arrived = refs[:-1], refs[-1]
    known = fill.shape[0]
    arrived[:known] = fill[...]
    arrived[known:] = first[...]

    def body(p, carry):
        pairs[p] = coupled(mine[p], arrived[spot[p]].T)
        return carry

    lax.fori_loop(0, mine.shape[0], body, 0, unroll=8)
    for hop, out in enumerate(outgoing):
        for slot in range(CAP):
            out[slot] = pairs[jnp.maximum(table[hop * CAP + slot], 0)]


def couple(table, spot, mine, fill, first, peers):
    pieces, tile, _ = mine.shape
    part = jax.ShapeDtypeStruct((CAP, tile, tile), BF)
    return pl.pallas_call(
        couple_kernel,
        out_shape=(jax.ShapeDtypeStruct((pieces, tile, tile), BF),) + (part,) * peers,
        grid_spec=pltpu.PrefetchScalarGridSpec(
            num_scalar_prefetch=2,
            in_specs=[WHOLE] * 3,
            out_specs=(WHOLE,) * (1 + peers),
            scratch_shapes=[pltpu.VMEM((fill.shape[0] + first.shape[0], tile, tile), BF)],
        ),
        compiler_params=SMALL,
        name="couple",
    )(table, spot, mine, fill, first)


def span(index, tile):
    return slice(index * tile, (index + 1) * tile)


def interior_kernel(spot, held, inverse, *refs):
    parts, (out, arrived) = refs[:-2], refs[-2:]
    step = pl.program_id(0)
    tile = arrived.shape[1]

    @pl.when(step == 0)
    def _():
        start = 0
        for part in parts:
            arrived[start : start + part.shape[0]] = part[...]
            start += part.shape[0]

    for row in range(INNER):
        for col in range(INNER):
            rows, cols = span(row, tile), span(col, tile)
            other = arrived[spot[step * INNER * INNER + row * INNER + col]].T
            value = coupled(held[step, rows, cols], other).astype(F32)
            out[0, rows, cols] = (value * inverse[step, rows, cols]).astype(BF)


def finish_interior(spot, held, inverse, *parts):
    channels, block, _ = held.shape
    tile = block // 4
    edge = INNER * tile
    return pl.pallas_call(
        interior_kernel,
        out_shape=jax.ShapeDtypeStruct(held.shape, BF),
        grid_spec=pltpu.PrefetchScalarGridSpec(
            num_scalar_prefetch=1,
            grid=(channels,),
            in_specs=[WHOLE] * (2 + len(parts)),
            out_specs=pl.BlockSpec((1, edge, edge), lambda s, *_: (s, 0, 0)),
            scratch_shapes=[pltpu.VMEM((sum(part.shape[0] for part in parts), tile, tile), BF)],
        ),
        compiler_params=SMALL,
        name="interior",
    )(spot, held, inverse, *parts)


def border_tiles(channel, held, inverse, parts, out, right_out, bottom_out, right_sem, bottom_sem):
    tile = right_out.shape[2]
    half = tile // 2
    edge = INNER * tile
    copies = []
    for part, inner_at in [(part, at) for part in parts for at in range(part.shape[0])]:
        at = len(copies) // 2
        slot = channel[at]

        def joined(unit):
            window = slice(unit * half, (unit + 1) * half)
            return jnp.concatenate([part[inner_at, 0, window], part[inner_at, 1, window]], axis=0)

        def value(row, col, other):
            rows, cols = span(row, tile), span(col, tile)
            total = coupled(held[slot, rows, cols], other).astype(F32)
            return (total * inverse[slot, rows, cols]).astype(BF)

        for row in range(INNER + 1):
            right_out[at, span(row, tile)] = value(row, INNER, joined(row).T)
        copies.append(
            pltpu.make_async_copy(right_out.at[at], out.at[slot, :, pl.ds(edge, tile)], right_sem.at[at])
        )
        copies[-1].start()
        for col in range(INNER):
            bottom_out[at, :, span(col, tile)] = value(INNER, col, joined(INNER + 1 + col))
        copies.append(
            pltpu.make_async_copy(
                bottom_out.at[at], out.at[slot, pl.ds(edge, tile), pl.ds(0, edge)], bottom_sem.at[at]
            )
        )
        copies[-1].start()
    return copies


def border_scratch(count, block):
    tile = block // 4
    return [
        pltpu.VMEM((count, block, tile), BF),
        pltpu.VMEM((count, tile, INNER * tile), BF),
        pltpu.SemaphoreType.DMA((count,)),
        pltpu.SemaphoreType.DMA((count,)),
    ]


def border_kernel(channel, held, inverse, *refs):
    parts, (_, out, *scratch) = refs[:-6], refs[-6:]
    for copy in border_tiles(channel, held, inverse, parts, out, *scratch):
        copy.wait()


def finish_border(channel, held, inverse, shells, prior):
    count = sum(part.shape[0] for part in shells)
    return pl.pallas_call(
        border_kernel,
        out_shape=jax.ShapeDtypeStruct(prior.shape, BF),
        grid_spec=pltpu.PrefetchScalarGridSpec(
            num_scalar_prefetch=1,
            in_specs=[WHOLE] * (2 + len(shells)) + [ANY],
            out_specs=ANY,
            scratch_shapes=border_scratch(count, prior.shape[1]),
        ),
        input_output_aliases={3 + len(shells): 0},
        compiler_params=SMALL,
        name="border",
    )(channel, held, inverse, *shells, prior)


def finale_kernel(channel, listed, table, held, inverse, shells, pairs, *refs):
    incoming, (_, out, mates, made, sem, *scratch) = refs[:-9], refs[-9:]
    pieces, tile, _ = pairs.shape
    copies = border_tiles(channel, held, inverse, (shells,), out, *scratch)
    for hop, part in enumerate(incoming):
        for slot in range(CAP):
            piece = table[hop * CAP + slot]
            mates[jnp.where(piece < 0, pieces, piece)] = part[slot]

    def body(p, carry):
        code = listed[p]
        slot = code // 16
        rows = pl.ds(pl.multiple_of((code % 16) // 4 * tile, tile), tile)
        cols = pl.ds(pl.multiple_of(code % 4 * tile, tile), tile)
        value = pairs[p].astype(F32) - mates[p].T.astype(F32)
        made[p] = (value * inverse[slot, rows, cols]).astype(BF)
        pltpu.make_async_copy(made.at[p], out.at[slot, rows, cols], sem).start()
        return carry

    lax.fori_loop(0, pieces, body, 0, unroll=8)
    for copy in copies:
        copy.wait()
    pltpu.make_async_copy(made, made, sem).wait()


def finale(channel, listed, table, held, inverse, shells, pairs, incoming, prior):
    pieces, tile, _ = pairs.shape
    arrays = (held, inverse, shells, pairs, *incoming)
    return pl.pallas_call(
        finale_kernel,
        out_shape=jax.ShapeDtypeStruct(prior.shape, BF),
        grid_spec=pltpu.PrefetchScalarGridSpec(
            num_scalar_prefetch=3,
            in_specs=[WHOLE] * len(arrays) + [ANY],
            out_specs=ANY,
            scratch_shapes=[
                pltpu.VMEM((pieces + 1, tile, tile), BF),
                pltpu.VMEM((pieces, tile, tile), BF),
                pltpu.SemaphoreType.DMA(()),
            ]
            + border_scratch(shells.shape[0], prior.shape[1]),
        ),
        input_output_aliases={3 + len(arrays): 0},
        compiler_params=SMALL,
        name="finale",
    )(channel, listed, table, *arrays, prior)


def exchange(amplitudes, coulomb, energies, orders, partner, listed, mate_piece):
    channels, _, _ = amplitudes.shape
    pieces = listed.shape[0]
    stride = lax.axis_size("chan") // 2
    peers = lax.axis_size("kin")
    route = [(i, i ^ stride) for i in range(2 * stride)]

    def swap(array):
        return lax.ppermute(array, "chan", route)

    wanted = swap(listed)
    res, fill, first, second, shells = residuals(orders, partner, wanted, amplitudes, coulomb)
    fill_in = swap(fill)
    first_in = swap(first)
    second_in = swap(second)
    shells_in = [swap(part) for part in shells]

    listed, partner, mate_piece, energies, res = lax.optimization_barrier(
        (listed, partner, mate_piece, energies, res)
    )
    held, inverse, mine = prepare(listed, energies, res)

    def total(hits):
        return jnp.sum(hits.astype(jnp.int32), axis=1)

    inner = INNER * INNER
    known = OPENING * inner
    slots = jnp.arange(channels, dtype=jnp.int32)
    partner_slot = partner % channels
    channel = jnp.sum(jnp.where(slots[:, None] == partner_slot[None, :], slots[None, :], 0), axis=1)

    def theirs(slot, row, col):
        other = jnp.sum(jnp.where(slot[:, None] == slots[None, :], partner_slot[None, :], 0), axis=1)
        return other * inner + col * INNER + row

    index = jnp.arange(pieces, dtype=jnp.int32)
    earlier = index[None, :] < index[:, None]
    piece_key = theirs(listed // 16, listed % 16 // 4, listed % 4)
    fresh = piece_key >= known
    piece_spot = jnp.where(fresh, known + total(earlier & fresh[None, :]), piece_key)
    tiles = jnp.arange(channels * inner, dtype=jnp.int32)
    key = theirs(tiles // inner, tiles % inner // INNER, tiles % INNER)
    plain = jnp.all(key[:, None] != piece_key[None, :], axis=1) & (key >= known)
    after = known + jnp.sum(fresh.astype(jnp.int32)) + total(plain[None, :] & (key[None, :] < key[:, None]))
    spot = jnp.minimum(jnp.where(key >= known, after, key), channels * inner - 1)

    target = mate_piece // pieces
    same = target[:, None] == target[None, :]
    out_rank = total(same & earlier)
    in_rank = total(same & (mate_piece[None, :] < mate_piece[:, None]))
    me = lax.axis_index("kin")
    places = jnp.arange(peers * CAP, dtype=jnp.int32)

    def table_of(hop, rank):
        hit = places[:, None] == ((hop + peers) % peers * CAP + rank)[None, :]
        return jnp.sum(jnp.where(hit, index[None, :] + 1, 0), axis=1) - 1

    out_table = table_of(target - me, out_rank)
    in_table = table_of(me - target, in_rank)
    mine, out_table, in_table, piece_spot, spot, channel = lax.optimization_barrier(
        (mine, out_table, in_table, piece_spot, spot, channel)
    )

    pairs, *outgoing = couple(out_table, piece_spot, mine, fill_in, first_in, peers)
    incoming = [outgoing[0]]
    for hop in range(1, peers):
        incoming.append(
            lax.ppermute(outgoing[hop], "kin", [(k, (k + hop) % peers) for k in range(peers)])
        )
    done = finish_interior(spot, held, inverse, fill_in, first_in, second_in)
    middle = channels - CLOSING
    done = finish_border(channel[:middle], held, inverse, shells_in[:2], done)
    return finale(channel[middle:], listed, in_table, held, inverse, shells_in[2], pairs, incoming, done)


def solution(mesh):
    return jax.shard_map(
        exchange,
        mesh=mesh,
        in_specs=(
            P(("chan", "kin"), None, None),
            P(("chan", "kin"), None, None),
            P(("chan", "kin"), None),
            P(("chan", "kin")),
            P(("chan", "kin")),
            P(("chan", "kin")),
            P(("chan", "kin")),
        ),
        out_specs=P(("chan", "kin"), None, None),
        check_vma=False,
    )
```
